32 devices in a mesh: groups: 2 (over x), wide: 16 (over z, y, core).
Axes of the slice: x: 2, y: 2, z: 4, core: 2. Of those that a mesh axis runs over, the one named last changes fastest.
Arguments:
- queries: bfloat16 [32, 16, 8, 128], P(('groups', 'wide')), parts along dimension 0, may hold values from -250 to 250
- keys_cache: bfloat16 [32, 16, 320, 128], P(('groups', 'wide')), parts along dimension 0, may hold values from -6 to 6
- values_cache: bfloat16 [32, 16, 320, 128], P(('groups', 'wide')), parts along dimension 0, may hold values from -6 to 6
- new_keys: bfloat16 [32, 16, 128], P(('groups', 'wide')), parts along dimension 0, may hold values from -6 to 6
- new_values: bfloat16 [32, 16, 128], P(('groups', 'wide')), parts along dimension 0, may hold values from -6 to 6
- lengths: int32 [64], P('groups'), parts along dimension 0, may hold values from 1 to 320, as said below
- assignment: int32 [64], P('groups'), parts along dimension 0, may hold values from 0 to 31, each once
- residual: bfloat16 [64, 8192], P('groups', 'wide'), parts along dimension 0, may hold values from -6 to 6
- w_out: bfloat16 [8192, 8192], P('wide'), may hold values from -0.0625 to 0.0625
- w_gate: bfloat16 [20480, 8192], P('wide'), may hold values from -0.0625 to 0.0625
- w_up: bfloat16 [20480, 8192], P('wide'), may hold values from -0.0625 to 0.0625
- w_down: bfloat16 [20480, 8192], P('wide'), may hold values from -0.0625 to 0.0625
- norm_gain: float32 [8192], P('wide'), may hold values from 0.25 to 1.75
Outputs:
- mixed: bfloat16 [64, 8192], P('groups', 'wide'), parts along dimension 0
The draws below stay inside these ranges and needn't reach their ends.
There are 2 independent parts, one for each index of `groups`. The reference program is written for one: setup_inputs(seed, part) draws one part's arguments, and reference() takes and returns one part's arrays. A program takes and returns all parts, laid end to end along the dimension named above; an argument that names none is the same for every part. Nothing has to cross between parts.
Inputs may be any that keep to these rules, and one draw needn't show every extreme that they name: `lengths`: every length is at least 1; one cache row has length exactly 320 in every draw. `assignment`: A permutation of the request numbers.
All inputs are finite; a program needn't handle non-finite values.
Results may differ from the reference program's by a relative error of at most 0.0052.
Values may be sent and summed in bfloat16 or wider, within the bound.
A program may use at most 128 MiB of HBM per device.

```python
import jax
import jax.numpy as jnp
from jax import lax

D = 8192
KV = 8
QPK = 8
HEAD = 128
FF = 20480
REQ_DEV = 16
LEN = 320
SHARDS = 2
SLOTS = 16
REQUESTS = 32


def draw_lengths(key, part):
    shard_caps = jax.random.randint(jax.random.fold_in(key, 11), (SHARDS,), LEN // 4, LEN + 1)
    raw_draw = jax.random.randint(jax.random.fold_in(key, 12), (SHARDS, REQ_DEV), 0, 1 << 20)
    drawn_lengths = (raw_draw % shard_caps[:, None] + 1).reshape(SHARDS * REQ_DEV)
    chosen_row = jax.random.randint(jax.random.fold_in(key, 13), (), 0, SHARDS * REQ_DEV)
    row_number = jnp.arange(SHARDS * REQ_DEV, dtype=jnp.int32)
    return jnp.where(row_number == chosen_row, LEN, drawn_lengths).astype(jnp.int32)


def draw_queries(key, part):
    drawn_values = jax.random.normal(key, (SLOTS, REQ_DEV, QPK, HEAD), jnp.float32)
    drawn_values = jnp.clip(drawn_values, -6.0, 6.0)
    return drawn_values.astype(jnp.bfloat16)


def with_spikes(drawn, stream_key, source, target, shards_of, factor):
    owner, partner = [(jnp.arange(drawn.shape[dim]) // (drawn.shape[dim] // shards_of)).reshape([-1 if axis == dim else 1 for axis in range(drawn.ndim)]) for dim in (source, target)]
    chosen = jax.random.permutation(stream_key, shards_of)[partner]
    strong = (owner == chosen) | (owner == (partner + shards_of // 2) % shards_of)
    return jnp.where(strong, factor * drawn, drawn)


def block_levels(own_key, dims, cuts, low, high):
    gain = 1.0
    for dim, shards_of in cuts:
        heights = jax.random.uniform(jax.random.fold_in(jax.random.fold_in(own_key, 6), dim), (shards_of,), jnp.float32, low / len(cuts), high / len(cuts))
        gain = gain * jnp.repeat(jnp.exp(heights), dims[dim] // shards_of).reshape((-1,) + (1,) * (len(dims) - 1 - dim))
    return gain


def normal_values(key, shape, scale, most, shards=(), kind=jnp.bfloat16):
    drawn = jax.random.normal(key, shape, jnp.float32) * scale
    if len(shards) > 0:
        drawn = block_levels(key, shape, shards, -0.22, 0.18) * drawn
    return jnp.clip(drawn, min=-most, max=most).astype(kind)


def heavy_noise(stream_key, shape, scale, most, shards, heavy, kind=jnp.bfloat16):
    entries = scale * jax.random.normal(stream_key, shape, jnp.float32)
    if shards:
        entries = entries * block_levels(stream_key, shape, shards, -0.22, 0.18)
    return jnp.clip(with_spikes(entries, jax.random.fold_in(stream_key, 3), *heavy), -most, most).astype(kind)


def setup_inputs(seed: int = 0, part: int = 0) -> dict:
    seeds = jax.random.split(jax.random.key(seed), 14)
    own_keys = jax.random.split(jax.random.fold_in(seeds[13], part), 14)
    queries = draw_queries(jax.random.fold_in(jax.random.fold_in(seeds[13], part), 71), part)
    keys_cache = normal_values(own_keys[1], (SLOTS, REQ_DEV, LEN, HEAD), 1.0, 6.0, ((0, 16),))
    values_cache = normal_values(own_keys[2], (SLOTS, REQ_DEV, LEN, HEAD), 1.0, 6.0, ((0, 16),))
    new_keys = normal_values(own_keys[3], (SLOTS, REQ_DEV, HEAD), 1.0, 6.0, ((0, 16),))
    new_values = normal_values(own_keys[4], (SLOTS, REQ_DEV, HEAD), 1.0, 6.0, ((0, 16),))
    lengths = draw_lengths(jax.random.fold_in(jax.random.fold_in(seeds[13], part), 71), part)
    assignment = jax.random.permutation(own_keys[6], REQUESTS).astype(jnp.int32)
    residual = normal_values(own_keys[7], (REQUESTS, D), 1.0, 6.0, ((1, 16),))
    w_out = normal_values(seeds[8], (D, D), D ** -0.5, 0.0625, ((0, 16),))
    w_gate = normal_values(seeds[9], (FF, D), D ** -0.5, 0.0625, ((0, 16),))
    w_up = normal_values(seeds[10], (FF, D), D ** -0.5, 0.0625, ((0, 16),))
    w_down = heavy_noise(seeds[11], (FF, D), FF ** -0.5, 0.0625, ((0, 16),), (0, 1, 16, 2.0))
    norm_gain = jnp.clip(1.0 + 0.15 * jax.random.normal(seeds[12], (D,), jnp.float32), 0.25, 1.75)
    return dict(queries=queries, keys_cache=keys_cache, values_cache=values_cache, new_keys=new_keys, new_values=new_values, lengths=lengths, assignment=assignment, residual=residual, w_out=w_out, w_gate=w_gate, w_up=w_up, w_down=w_down, norm_gain=norm_gain)


def attend_slot(query_rows, keys_local, values_local, key_new, value_new, lens_local):
    inv_scale = HEAD ** (-0.5)
    scores = jnp.einsum('rqe,rpe->rqp', query_rows.astype(jnp.float32), keys_local.astype(jnp.float32)) * inv_scale
    position = jnp.arange(LEN, dtype=jnp.int32)
    scores = jnp.where(position[None, None, :] < lens_local[:, None, None], scores, -1e+30)
    own_score = jnp.einsum('rqe,re->rq', query_rows.astype(jnp.float32), key_new.astype(jnp.float32)) * inv_scale
    top_score = jnp.maximum(lax.optimization_barrier(jnp.max(scores, axis=2)), own_score)
    weights = jnp.exp(scores - top_score[:, :, None])
    own_weight = jnp.exp(own_score - top_score)
    total_sum = lax.optimization_barrier(jnp.sum(weights, axis=2)) + own_weight
    weights_low = lax.optimization_barrier(weights.astype(jnp.bfloat16)).astype(jnp.float32)
    own_low = lax.optimization_barrier(own_weight.astype(jnp.bfloat16)).astype(jnp.float32)
    weighted = jnp.einsum('rqp,rpe->rqe', weights_low, values_local.astype(jnp.float32))
    weighted = weighted + own_low[:, :, None] * value_new.astype(jnp.float32)[:, None, :]
    return (weighted / total_sum[:, :, None]).astype(jnp.bfloat16).reshape(REQ_DEV, QPK * HEAD)

def contract_last(left, right):
    return lax.dot_general(left, right, (((1,), (1,)), ((), ())), preferred_element_type=jnp.float32)

def reference(queries, keys_cache, values_cache, new_keys, new_values, lengths, assignment, residual, w_out, w_gate, w_up, w_down, norm_gain):
    slot_lengths = jnp.broadcast_to(lengths.reshape(SHARDS, 1, REQ_DEV), (SHARDS, KV, REQ_DEV)).reshape(SLOTS, REQ_DEV)
    per_slot = lax.map(lambda items: attend_slot(*items), (queries, keys_cache, values_cache, new_keys, new_values, slot_lengths))
    attended = per_slot.reshape(SHARDS, KV, REQ_DEV, QPK * HEAD).transpose(0, 2, 1, 3).reshape(REQUESTS, D)
    by_request = jnp.zeros((REQUESTS, D), jnp.bfloat16).at[assignment.astype(jnp.int32)].set(attended)
    state = residual.astype(jnp.float32) + contract_last(by_request, w_out)
    inv_rms = lax.rsqrt(lax.optimization_barrier(jnp.mean(state * state, axis=1)) + 1e-05)
    normed = (state * inv_rms[:, None] * norm_gain[None, :]).astype(jnp.bfloat16)
    gate_val = contract_last(normed, w_gate)
    up_val = contract_last(normed, w_up)
    hidden = (jax.nn.silu(gate_val) * up_val).astype(jnp.bfloat16)
    return (state + jnp.dot(hidden, w_down, preferred_element_type=jnp.float32)).astype(jnp.bfloat16)
```

```python
import functools
import math

import jax
import jax.numpy as jnp
from jax import lax
from jax.experimental import pallas as pl
from jax.experimental.pallas import tpu as pltpu
from jax.sharding import PartitionSpec as P

D = 8192
KV = 8


KEY_BLOCK = 64
EPSILON = 1e-05
NEG_FILL = -1e30


def contract_last(left, right):
    return lax.dot_general(
        left, right, (((1,), (1,)), ((), ())), preferred_element_type=jnp.float32
    )


def masked_scores(query_rows, keys_local, lens_local, block_index, inv_scale):
    key_block = lax.dynamic_slice_in_dim(keys_local, block_index * KEY_BLOCK, KEY_BLOCK, 1)
    scores = (
        jnp.einsum("rqe,rpe->rqp", query_rows, key_block, preferred_element_type=jnp.float32)
        * inv_scale
    )
    position = block_index * KEY_BLOCK + lax.broadcasted_iota(jnp.int32, scores.shape, 2)
    return jnp.where(position < lens_local[:, None, None], scores, NEG_FILL)


SLOT_COUNT = 44
VMEM_BYTES = 67043328


def layer_kernel(
    n,
    lengths,
    assignment,
    queries,
    new_keys,
    new_values,
    residual,
    norm_gain,
    keys_hbm,
    values_hbm,
    w_out,
    w_gate,
    w_up,
    w_down,
    out,
    keys,
    values,
    slots,
    scores,
    weights,
    acc,
    heads,
    state,
    scaled,
    squares,
    gate_acc,
    up_acc,
    hidden,
    send_parts,
    recv_parts,
    own_part,
    cache_sems,
    slot_sems,
    head_send,
    head_recv,
    scaled_send,
    scaled_recv,
    square_send,
    square_recv,
    part_send,
    part_recv,
):
    me = lax.axis_index("wide")
    my_shard, my_group = me // KV, me % KV
    req_dev, qpk, head = queries.shape[1:]
    requests, cols = residual.shape
    units = w_gate.shape[0]
    shards = n // KV
    halves = qpk * head // cols
    extra = SLOT_COUNT - KV - 2 * n

    def source(k):
        return lax.rem(me - k + n, n)

    def target(k):
        return lax.rem(me + k, n)

    def col_block(index):
        return pl.ds(pl.multiple_of(index * cols, cols), cols)

    def out_fill(k, half):
        group = lax.rem(my_group - k + KV, KV)
        return pltpu.make_async_copy(
            w_out.at[:, col_block(group * halves + half)],
            slots.at[k, pl.ds(half * cols, cols)],
            slot_sems.at[k, half],
        )

    def gate_fill(k):
        slot = KV + 2 * k
        return pltpu.make_async_copy(
            w_gate.at[:, col_block(source(k))], slots.at[slot], slot_sems.at[slot, 0]
        )

    def up_fill(k):
        slot = KV + 2 * k + 1
        return pltpu.make_async_copy(
            w_up.at[:, col_block(source(k))], slots.at[slot], slot_sems.at[slot, 0]
        )

    def down_slot(k):
        return jnp.where(k < extra, KV + 2 * n + k, k - extra)

    def down_fill(k):
        slot = down_slot(k)
        return pltpu.make_async_copy(
            w_down.at[:, col_block(target(k + 1))], slots.at[slot], slot_sems.at[slot, 0]
        )

    def remote(src, dst, send_sem, recv_sem, device):
        return pltpu.make_async_remote_copy(
            src_ref=src,
            dst_ref=dst,
            send_sem=send_sem,
            recv_sem=recv_sem,
            device_id={"wide": device},
            device_id_type=pl.DeviceIdType.MESH,
        )

    def head_copy(k, owner):
        return remote(
            heads.at[owner], heads.at[owner], head_send.at[k], head_recv.at[owner], target(k)
        )

    def scaled_copy(k, owner):
        return remote(
            scaled.at[owner], scaled.at[owner], scaled_send.at[k], scaled_recv.at[owner], target(k)
        )

    def square_copy(k, owner):
        return remote(
            squares.at[owner],
            squares.at[owner],
            square_send.at[k],
            square_recv.at[owner],
            target(k),
        )

    def part_copy(k, owner):
        return remote(
            send_parts.at[k], recv_parts.at[owner], part_send.at[k], part_recv.at[owner], target(k)
        )

    def each(low, high, body):
        def step(k, carry):
            body(k)
            return carry

        lax.fori_loop(low, high, step, 0)

    key_copy = pltpu.make_async_copy(keys_hbm.at[0], keys, cache_sems.at[0])
    value_copy = pltpu.make_async_copy(values_hbm.at[0], values, cache_sems.at[1])
    key_copy.start()
    value_copy.start()

    @functools.partial(each, 0, KV)
    def _(k):
        for half in range(halves):
            out_fill(k, half).start()

    barrier = pltpu.get_barrier_semaphore()

    @functools.partial(each, 1, n)
    def _(k):
        pl.semaphore_signal(
            barrier,
            inc=1,
            device_id={"wide": target(k)},
            device_id_type=pl.DeviceIdType.MESH,
        )

    key_copy.wait()
    value_copy.wait()

    @functools.partial(each, 0, n)
    def _(k):
        gate_fill(k).start()
        up_fill(k).start()

    @functools.partial(each, 0, min(extra, n))
    def _(k):
        down_fill(k).start()

    inv_scale = 1.0 / math.sqrt(head)
    for row in range(req_dev):
        block = contract_last(queries[0, row], keys[row]) * inv_scale
        position = lax.broadcasted_iota(jnp.int32, block.shape, 1)
        scores[row] = jnp.where(
            position < lengths[my_shard * req_dev + row], block, NEG_FILL
        )
    own_score = (
        jnp.sum(
            queries[0].astype(jnp.float32) * new_keys[0].astype(jnp.float32)[:, None, :],
            axis=2,
            keepdims=True,
        )
        * inv_scale
    )
    all_scores = scores[...]
    top = jnp.maximum(jnp.max(all_scores, axis=2, keepdims=True), own_score)
    exps = jnp.exp(all_scores - top)
    own_weight = jnp.exp(own_score - top)
    total = jnp.sum(exps, axis=2, keepdims=True) + own_weight
    weights[...] = exps.astype(jnp.bfloat16)
    for row in range(req_dev):
        acc[row] = jnp.dot(weights[row], values[row], preferred_element_type=jnp.float32)
    own_low = own_weight.astype(jnp.bfloat16).astype(jnp.float32)
    own_term = own_low * new_values[0].astype(jnp.float32)[:, None, :]
    acc[...] = (acc[...] + own_term) / total
    for index in range(qpk):
        heads[me, :, index * head : (index + 1) * head] = acc[:, index, :].astype(jnp.bfloat16)

    pl.semaphore_wait(barrier, n - 1)

    @functools.partial(each, 1, n)
    def _(k):
        head_copy(k, me).start()

    request_row = lax.broadcasted_iota(jnp.int32, (requests, requests), 0)
    cache_col = lax.broadcasted_iota(jnp.int32, (requests, requests), 1)
    place = jnp.zeros((requests, requests), jnp.float32)
    for row in range(requests):
        place = jnp.where(
            jnp.logical_and(cache_col == row, request_row == assignment[row]), 1.0, place
        )
    state[...] = lax.dot_general(
        place.T.astype(jnp.bfloat16),
        residual[...],
        (((1,), (0,)), ((), ())),
        preferred_element_type=jnp.float32,
    )

    @functools.partial(each, 0, KV)
    def _(k):
        group = lax.rem(my_group - k + KV, KV)
        for half in range(halves):
            out_fill(k, half).wait()
        for shard in range(shards):
            owner = shard * KV + group

            @pl.when(owner != me)
            def _():
                head_copy(0, owner).wait_recv()

        rows = jnp.concatenate([heads[shard * KV + group] for shard in range(shards)], axis=0)
        term = state[...]
        for half in range(halves):
            term = term + contract_last(
                rows[:, half * cols : (half + 1) * cols],
                slots[k, half * cols : (half + 1) * cols, :],
            )
        state[...] = term

    my_state = state[...]
    scaled[me] = (my_state * norm_gain[...][None, :]).astype(jnp.bfloat16)
    row_sums = jnp.sum(my_state * my_state, axis=1, keepdims=True)
    diagonal = lax.broadcasted_iota(
        jnp.int32, (requests, squares.shape[2]), 0
    ) == lax.broadcasted_iota(jnp.int32, (requests, squares.shape[2]), 1)
    flat_sums = jnp.sum(jnp.where(diagonal, row_sums, 0.0), axis=0, keepdims=True)
    squares[me] = jnp.broadcast_to(flat_sums, squares.shape[1:])

    @functools.partial(each, 1, n)
    def _(k):
        scaled_copy(k, me).start()
        square_copy(k, me).start()

    @functools.partial(each, extra, min(extra + KV, n))
    def _(k):
        down_fill(k).start()

    gate_acc[...] = jnp.zeros_like(gate_acc)
    up_acc[...] = jnp.zeros_like(up_acc)

    @functools.partial(each, 0, n)
    def _(k):
        owner = source(k)
        gate_fill(k).wait()
        up_fill(k).wait()

        @pl.when(k > 0)
        def _():
            scaled_copy(0, owner).wait_recv()

        piece = scaled[owner]
        gate_acc[...] += contract_last(piece, slots[KV + 2 * k])
        up_acc[...] += contract_last(piece, slots[KV + 2 * k + 1])

        for step in range(2):
            later = extra + KV + 2 * k + step

            @pl.when(later < n)
            def _():
                down_fill(later).start()

    @functools.partial(each, 1, n)
    def _(k):
        square_copy(0, source(k)).wait_recv()

    sum_squares = jnp.sum(squares[...], axis=0)[:1]
    row_squares = jnp.sum(jnp.where(diagonal, sum_squares, 0.0), axis=1, keepdims=True)
    inv_rms = lax.rsqrt(row_squares / (n * cols) + EPSILON)
    gate_val = gate_acc[...] * inv_rms
    hidden[...] = (gate_val * jax.nn.sigmoid(gate_val) * (up_acc[...] * inv_rms)).astype(
        jnp.bfloat16
    )

    @functools.partial(each, 0, n)
    def _(k):
        down_fill(k).wait()
        part = jnp.dot(hidden[...], slots[down_slot(k)], preferred_element_type=jnp.float32)

        @pl.when(k < n - 1)
        def _():
            send_parts[k + 1] = part.astype(jnp.bfloat16)
            part_copy(k + 1, me).start()

        @pl.when(k == n - 1)
        def _():
            own_part[...] = part + state[...]

    @functools.partial(each, 1, n)
    def _(k):
        owner = source(k)
        part_copy(0, owner).wait_recv()
        own_part[...] += recv_parts[owner].astype(jnp.float32)

    out[...] = jnp.dot(
        place.astype(jnp.bfloat16),
        own_part[...].astype(jnp.bfloat16),
        preferred_element_type=jnp.float32,
    ).astype(jnp.bfloat16)

    @functools.partial(each, 1, n)
    def _(k):
        head_copy(k, me).wait_send()
        scaled_copy(k, me).wait_send()
        square_copy(k, me).wait_send()
        part_copy(k, me).wait_send()


def kernel_fits(n, queries, keys_cache, residual, w_gate):
    requests, cols = residual.shape
    units = w_gate.shape[0]
    feats = queries.shape[2] * queries.shape[3]
    slot_bytes = SLOT_COUNT * units * cols * 2
    return (
        n % KV == 0
        and cols % 128 == 0
        and units % 128 == 0
        and feats % cols == 0
        and feats <= units
        and requests <= 128
        and KV + 2 * n <= SLOT_COUNT
        and slot_bytes + 4 * keys_cache.size + (6 << 20) <= VMEM_BYTES
    )


def fused_layer(
    n,
    queries,
    keys_cache,
    values_cache,
    new_keys,
    new_values,
    lengths,
    assignment,
    residual,
    w_out,
    w_gate,
    w_up,
    w_down,
    norm_gain,
):
    req_dev, qpk, head = queries.shape[1:]
    positions = keys_cache.shape[2]
    requests, cols = residual.shape
    units = w_gate.shape[0]
    low, full = jnp.bfloat16, jnp.float32
    smem = pl.BlockSpec(memory_space=pltpu.SMEM)
    vmem = pl.BlockSpec(memory_space=pltpu.VMEM)
    anywhere = pl.BlockSpec(memory_space=pl.ANY)
    dma = pltpu.SemaphoreType.DMA
    return pl.pallas_call(
        functools.partial(layer_kernel, n),
        out_shape=jax.ShapeDtypeStruct((requests, cols), low),
        in_specs=[smem] * 2 + [vmem] * 5 + [anywhere] * 6,
        out_specs=vmem,
        scratch_shapes=[
            pltpu.VMEM((req_dev, positions, head), low),
            pltpu.VMEM((req_dev, positions, head), low),
            pltpu.VMEM((SLOT_COUNT, units, cols), low),
            pltpu.VMEM((req_dev, qpk, positions), full),
            pltpu.VMEM((req_dev, qpk, positions), low),
            pltpu.VMEM((req_dev, qpk, head), full),
            pltpu.VMEM((n, req_dev, qpk * head), low),
            pltpu.VMEM((requests, cols), full),
            pltpu.VMEM((n, requests, cols), low),
            pltpu.VMEM((n, 8, 128), full),
            pltpu.VMEM((requests, units), full),
            pltpu.VMEM((requests, units), full),
            pltpu.VMEM((requests, units), low),
            pltpu.VMEM((n, requests, cols), low),
            pltpu.VMEM((n, requests, cols), low),
            pltpu.VMEM((requests, cols), full),
            dma((2,)),
            dma((SLOT_COUNT, max(2, qpk * head // cols))),
        ]
        + [dma((n,))] * 8,
        compiler_params=pltpu.CompilerParams(
            collective_id=0, has_side_effects=True, vmem_limit_bytes=VMEM_BYTES
        ),
    )(
        lengths,
        assignment,
        queries,
        new_keys,
        new_values,
        residual,
        norm_gain,
        keys_cache,
        values_cache,
        w_out,
        w_gate,
        w_up,
        w_down,
    )


def on_device(
    queries,
    keys_cache,
    values_cache,
    new_keys,
    new_values,
    lengths,
    assignment,
    residual,
    w_out,
    w_gate,
    w_up,
    w_down,
    norm_gain,
):
    n = lax.axis_size("wide")
    if kernel_fits(n, queries, keys_cache, residual, w_gate):
        return fused_layer(
            n,
            queries,
            keys_cache,
            values_cache,
            new_keys,
            new_values,
            lengths,
            assignment,
            residual,
            w_out,
            w_gate,
            w_up,
            w_down,
            norm_gain,
        )
    my_index = lax.axis_index("wide")
    my_shard = my_index // KV
    req_dev = queries.shape[1]
    query_rows = queries[0]
    keys_local = keys_cache[0]
    values_local = values_cache[0]
    lens_local = lax.dynamic_slice_in_dim(lengths, my_shard * req_dev, req_dev)
    inv_scale = 1.0 / math.sqrt(query_rows.shape[2])
    own_score = (
        jnp.einsum("rqe,re->rq", query_rows, new_keys[0], preferred_element_type=jnp.float32)
        * inv_scale
    )
    block_count = (jnp.max(lens_local) + KEY_BLOCK - 1) // KEY_BLOCK

    def find_top(block_index, running):
        return jnp.maximum(
            running,
            jnp.max(
                masked_scores(query_rows, keys_local, lens_local, block_index, inv_scale), axis=2
            ),
        )

    top_score = lax.fori_loop(0, block_count, find_top, own_score)
    own_weight = jnp.exp(own_score - top_score)
    own_low = lax.optimization_barrier(own_weight.astype(jnp.bfloat16)).astype(jnp.float32)
    start_state = (own_weight, own_low[:, :, None] * new_values[0].astype(jnp.float32)[:, None, :])

    def accumulate(block_index, state_pair):
        total_sum, weighted = state_pair
        weights = jnp.exp(
            masked_scores(query_rows, keys_local, lens_local, block_index, inv_scale)
            - top_score[:, :, None]
        )
        value_block = lax.dynamic_slice_in_dim(values_local, block_index * KEY_BLOCK, KEY_BLOCK, 1)
        weighted = weighted + jnp.einsum(
            "rqp,rpe->rqe",
            weights.astype(jnp.bfloat16),
            value_block,
            preferred_element_type=jnp.float32,
        )
        return (total_sum + jnp.sum(weights, axis=2), weighted)

    total_sum, weighted = lax.fori_loop(0, block_count, accumulate, start_state)
    attended = (weighted / total_sum[:, :, None]).astype(jnp.bfloat16).reshape(1, req_dev, -1)
    feat_width = attended.shape[2]
    head_piece = lax.all_gather(attended, "wide", axis=0, tiled=True)

    def one_source(offset, running):
        source_shard = offset // KV
        source_group = offset % KV
        request_ids = lax.dynamic_slice_in_dim(assignment, source_shard * req_dev, req_dev)
        out_cols = lax.dynamic_slice_in_dim(w_out, source_group * feat_width, feat_width, 1)
        source_rows = lax.dynamic_index_in_dim(head_piece, offset, 0, keepdims=False)
        term = contract_last(source_rows, out_cols)
        return running.at[request_ids].add(term)

    projected = lax.fori_loop(
        0,
        head_piece.shape[0],
        one_source,
        jnp.zeros((assignment.shape[0], w_out.shape[0]), jnp.float32),
    )
    hidden_state = residual.astype(jnp.float32) + projected
    row_squares = lax.psum(jnp.sum(hidden_state * hidden_state, axis=1), "wide")
    inv_rms = lax.rsqrt(row_squares / D + EPSILON)
    normed_cols = (hidden_state * inv_rms[:, None] * norm_gain[None, :]).astype(jnp.bfloat16)
    normed_piece = lax.all_gather(normed_cols, "wide", axis=1, tiled=True)
    gate_val = contract_last(normed_piece, w_gate)
    up_val = contract_last(normed_piece, w_up)
    activated = (jax.nn.silu(gate_val) * up_val).astype(jnp.bfloat16)
    down_terms = jnp.dot(activated, w_down, preferred_element_type=jnp.float32)
    down_part = lax.psum_scatter(down_terms, "wide", scatter_dimension=1, tiled=True)
    return (hidden_state + down_part).astype(jnp.bfloat16)


def solution(mesh):
    placed = (
        P(("groups", "wide"), None, None, None),
        P(("groups", "wide"), None, None, None),
        P(("groups", "wide"), None, None, None),
        P(("groups", "wide"), None, None),
        P(("groups", "wide"), None, None),
        P("groups"),
        P("groups"),
        P("groups", "wide"),
        P("wide", None),
        P("wide", None),
        P("wide", None),
        P("wide", None),
        P("wide"),
    )
    return jax.shard_map(
        on_device, mesh=mesh, in_specs=placed, out_specs=P("groups", "wide"), check_vma=False
    )
```
